32 devices in a mesh: blk: 8 (over z, x), grp: 4 (over y, core).
Axes of the slice: x: 2, y: 2, z: 4, core: 2. Of those that a mesh axis runs over, the one named last changes fastest.
Arguments:
- image_student: bfloat16 [8, 4, 256, 768], P('blk', 'grp'), may hold values from -6 to 6
- image_teacher: bfloat16 [8, 4, 256, 1152], P('blk', 'grp'), may hold values from -6 to 6
- text_student: bfloat16 [8, 4, 256, 768], P('blk', 'grp'), may hold values from -6 to 6
- text_teacher: bfloat16 [8, 4, 256, 1152], P('blk', 'grp'), may hold values from -6 to 6
- pair_ids: int32 [8, 4, 256], P('blk', 'grp'), may hold values from 0 to 511
Outputs:
- image_grad: float32 [8, 4, 256, 768], P('blk', 'grp')
- text_grad: float32 [8, 4, 256, 768], P('blk', 'grp')
- bias_grad: float32 [], replicated
The draws below stay inside these ranges and needn't reach their ends.
All inputs are finite; a program needn't handle non-finite values.
Results may differ from the reference program's by a relative error of at most 0.0021.
Values may be sent and summed in bfloat16 or wider, within the bound.
A program may use at most 64 MiB of HBM per device.

```python
import math
import jax
import jax.numpy as jnp
from jax import lax

DS = 768
DT = 1152
P_SIZE = 256
WINDOW = 4
NB = 8
NG = 4
N_BLK = 8
N_GRP = 4


def touch_ends(values, rng, smallest, high):
    longest = values.shape.index(max(values.shape))
    spots = []
    for shift in (0, 1):
        where = [jax.random.randint(jax.random.fold_in(rng, axis), (), 0, length) for axis, length in enumerate(values.shape)]
        where[longest] = (where[longest] + shift) % values.shape[longest]
        spots.append(tuple(where))
    return values.at[spots[0]].set(smallest).at[spots[1]].set(high)


def block_scale(own_key, extent, split, least, high):
    loudness, own = 1.0, jax.random.fold_in(own_key, 6)
    for axis_at, blocks in split:
        steps = jnp.exp(jax.random.uniform(jax.random.fold_in(own, axis_at), (blocks,), jnp.float32, least / len(split), high / len(split)))
        loudness = loudness * jnp.repeat(steps, extent[axis_at] // blocks).reshape([-1 if axis == axis_at else 1 for axis in range(len(extent))])
    return loudness


def bell_draw(stream_key, extent, spread, most, split=(), dtype=jnp.bfloat16):
    factor_of = block_scale(stream_key, extent, split, -0.22, 0.18) if split else 1.0
    entries = jax.random.normal(stream_key, extent, jnp.float32) * spread * factor_of
    return jnp.minimum(jnp.maximum(entries, -most), most).astype(dtype)


def setup_inputs(seed: int = 0) -> dict:
    streams_of = jax.random.split(jax.random.key(seed), 6)
    image_student = bell_draw(streams_of[0], (NB, NG, P_SIZE, DS), 1.0, 6.0, ((0, 8), (1, 4)))
    image_teacher = bell_draw(streams_of[1], (NB, NG, P_SIZE, DT), 1.0, 6.0, ((0, 8), (1, 4)))
    text_student = bell_draw(streams_of[2], (NB, NG, P_SIZE, DS), 1.0, 6.0, ((0, 8), (1, 4)))
    text_teacher = bell_draw(streams_of[3], (NB, NG, P_SIZE, DT), 1.0, 6.0, ((0, 8), (1, 4)))
    pair_ids = touch_ends(jax.random.randint(streams_of[4], (NB, NG, P_SIZE), 0, 2 * P_SIZE), jax.random.fold_in(streams_of[4], 1), 0, (2 * P_SIZE) - 1).astype(jnp.int32)
    return dict(image_student=image_student, image_teacher=image_teacher, text_student=text_student, text_teacher=text_teacher, pair_ids=pair_ids)


def reference(image_student, image_teacher, text_student, text_teacher, pair_ids):
    scale_s = 2.0 / math.sqrt(DS)
    scale_t = 2.0 / math.sqrt(DT)
    img_stu = image_student.astype(jnp.float32)
    img_tea = image_teacher.astype(jnp.float32)
    image_grad = jnp.zeros(img_stu.shape, jnp.float32)
    text_grad = jnp.zeros(img_stu.shape, jnp.float32)
    total = jnp.float32(0.0)
    for offset in range(WINDOW):
        txt_stu = jnp.roll(text_student, offset, axis=0).astype(jnp.float32)
        txt_tea = jnp.roll(text_teacher, offset, axis=0).astype(jnp.float32)
        txt_ids = jnp.roll(pair_ids, offset, axis=0)
        scores = jnp.einsum('bgpd,bgqd->bgpq', img_stu, txt_stu) * scale_s - 1.0
        teacher = jnp.einsum('bgpd,bgqd->bgpq', img_tea, txt_tea) * scale_t - 1.0
        match = (pair_ids[:, :, :, None] == txt_ids[:, :, None, :]).astype(jnp.float32)
        weights = jax.nn.sigmoid(scores) - 0.5 * jax.nn.sigmoid(teacher) - 0.5 * match
        total = total + jnp.sum(weights)
        rounded = lax.optimization_barrier(weights.astype(jnp.bfloat16)).astype(jnp.float32)
        image_grad = image_grad + jnp.einsum('bgpq,bgqd->bgpd', rounded, txt_stu) * scale_s
        partial_txt = jnp.einsum('bgpq,bgpd->bgqd', rounded, img_stu) * scale_s
        text_grad = text_grad + jnp.roll(partial_txt, -offset, axis=0)
    count = float(N_BLK * N_GRP * WINDOW * P_SIZE * P_SIZE)
    return (image_grad, text_grad, total / count)
```

```python
import functools
import math

import jax
import jax.numpy as jnp
from jax import lax
from jax.experimental import pallas as pl
from jax.experimental.pallas import tpu as pltpu
from jax.sharding import PartitionSpec as P

MESH = pl.DeviceIdType.MESH
WINDOW = 4
CHUNKS = 4
PLAIN = ("nnnnffff", "")
NEAR_WRAPS = ("ffff", "nnnn")
FAR_WRAPS = ("nnnn", "ffff")


def dot_nt(a, b):
    return lax.dot_general(a, b, (((1,), (1,)), ((), ())), preferred_element_type=jnp.float32)


def dot_tn(a, b):
    return lax.dot_general(a, b, (((0,), (0,)), ((), ())), preferred_element_type=jnp.float32)


def dot_nn(a, b):
    return jnp.dot(a, b, preferred_element_type=jnp.float32)


def fold(w):
    w = jnp.sum(w.reshape(w.shape[0] // 8, 8, w.shape[1]), axis=0)
    out = w[:, 0:128]
    for at in range(128, w.shape[1], 128):
        out = out + w[:, at : at + 128]
    return out


def kernel(
    n_blk,
    n_grp,
    ds,
    inv_count,
    img_stu,
    img_tea,
    txt_stu,
    txt_tea,
    ids,
    acc_far,
    acc_near,
    out_bias,
    far,
    near,
    own_ids,
    far_in,
    near_in,
    far_ids_in,
    near_ids_in,
    part,
    pf_out,
    pn_out,
    pf_in,
    pn_in,
    total,
    stage1_own,
    stage1,
    stage2_own,
    stage2,
    local_sem,
    far_send,
    far_recv,
    near_send,
    near_recv,
    ids_send,
    ids_recv,
    pf_send,
    pf_recv,
    pn_send,
    pn_recv,
    s1_send,
    s1_recv,
    s2_send,
    s2_recv,
    up_sem,
    down_sem,
):
    b = lax.axis_index("blk")
    g = lax.axis_index("grp")
    size = far.shape[0]
    dt = far.shape[1] - ds
    role = lax.rem(g, 2)
    step = 1 - 2 * role
    far_to = lax.rem(b + 2 * step + 2 * n_blk, n_blk)
    far_from = lax.rem(b - 2 * step + 2 * n_blk, n_blk)
    near_to = lax.rem(b - step + n_blk, n_blk)
    near_from = lax.rem(b + step + n_blk, n_blk)

    def at_blk(i):
        return {"blk": i, "grp": g}

    def loads(f_stu, f_tea, n_stu, n_tea):
        return [
            pltpu.make_async_copy(f_stu, far.at[:, pl.ds(0, ds)], local_sem.at[0]),
            pltpu.make_async_copy(f_tea, far.at[:, pl.ds(ds, dt)], local_sem.at[1]),
            pltpu.make_async_copy(n_stu, near.at[:, pl.ds(0, ds)], local_sem.at[2]),
            pltpu.make_async_copy(n_tea, near.at[:, pl.ds(ds, dt)], local_sem.at[3]),
        ]

    @pl.when(role == 0)
    def _():
        for c in loads(txt_stu, txt_tea, img_stu, img_tea):
            c.start()

    @pl.when(role == 1)
    def _():
        for c in loads(img_stu, img_tea, txt_stu, txt_tea):
            c.start()

    ids_load = pltpu.make_async_copy(ids, own_ids, local_sem.at[4])
    ids_load.start()

    has_up, has_down = b + 2 < n_blk, b >= 2
    links = ((1, b + 1 < n_blk), (2, has_up), (-1, b >= 1), (-2, has_down))
    barrier = pltpu.get_barrier_semaphore()
    expected = jnp.int32(n_grp - 1)
    for offset, present in links:
        expected = expected + present.astype(jnp.int32)

        @pl.when(present)
        def _():
            pl.semaphore_signal(
                barrier, inc=1, device_id=at_blk(b + offset), device_id_type=MESH
            )

    for k in range(1, n_grp):
        pl.semaphore_signal(
            barrier,
            inc=1,
            device_id={"blk": b, "grp": lax.rem(g + k, n_grp)},
            device_id_type=MESH,
        )
    for c in loads(txt_stu, txt_tea, img_stu, img_tea):
        c.wait()
    ids_load.wait()
    pl.semaphore_wait(barrier, expected)

    def remote(src, dst, send, recv, to):
        return pltpu.make_async_remote_copy(
            src_ref=src, dst_ref=dst, send_sem=send, recv_sem=recv,
            device_id=to, device_id_type=MESH,
        )

    each = size // CHUNKS
    ids_f = remote(own_ids, far_ids_in, ids_send.at[0], ids_recv.at[0], at_blk(far_to))
    ids_n = remote(own_ids, near_ids_in, ids_send.at[1], ids_recv.at[1], at_blk(near_to))
    near_copies = [
        remote(
            near.at[pl.ds(j * each, each)], near_in.at[pl.ds(j * each, each)],
            near_send.at[j], near_recv.at[j], at_blk(near_to),
        )
        for j in range(CHUNKS)
    ]
    far_copies = [
        remote(
            far.at[pl.ds(i * each, each)], far_in.at[pl.ds(i * each, each)],
            far_send.at[i], far_recv.at[i], at_blk(far_to),
        )
        for i in range(CHUNKS)
    ]
    near_wraps = jnp.where(role == 0, b == 0, b == n_blk - 1)
    far_wraps = jnp.where(role == 0, jnp.logical_not(has_up), jnp.logical_not(has_down))

    def begin(order, done=""):
        sent = {"n": done.count("n"), "f": done.count("f")}
        for kind in order:
            ids_copy, copies = (ids_n, near_copies) if kind == "n" else (ids_f, far_copies)
            if sent[kind] == 0:
                ids_copy.start()
            copies[sent[kind]].start()
            sent[kind] += 1

    plain = jnp.logical_not(jnp.logical_or(near_wraps, far_wraps))
    cases = ((plain, PLAIN), (near_wraps, NEAR_WRAPS), (far_wraps, FAR_WRAPS))
    for case, (at_once, _) in cases:

        @pl.when(case)
        def _():
            begin(at_once)

    def tell(sem, offset):
        pl.semaphore_signal(sem, inc=1, device_id=at_blk(b + offset), device_id_type=MESH)

    def pass_up():
        @pl.when(has_down)
        def _():
            pl.semaphore_wait(up_sem, 1)

        @pl.when(has_up)
        def _():
            tell(up_sem, 2)

    def pass_down():
        @pl.when(has_up)
        def _():
            pl.semaphore_wait(down_sem, 1)

        @pl.when(has_down)
        def _():
            tell(down_sem, -2)

    lower = b < n_blk // 2

    @pl.when(lower)
    def _():
        pass_up()
        pass_down()

    @pl.when(jnp.logical_not(lower))
    def _():
        pass_down()
        pass_up()

    for case, (at_once, after) in cases:

        @pl.when(case)
        def _():
            begin(after, at_once)

    scale_s = 2.0 / math.sqrt(ds)
    scale_t = 2.0 / math.sqrt(dt)

    def as_column(row):
        return jnp.transpose(jnp.broadcast_to(row, (128, row.shape[1])))[:, 0:1]

    def weigh(f, n, f_id, n_id):
        s = dot_nt(f[:, :ds], n[:, :ds]) * (0.5 * scale_s) - 0.5
        q = dot_nt(f[:, ds:], n[:, ds:]) * (0.5 * scale_t) - 0.5
        shift = jnp.where(f_id == n_id, -0.25, 0.25)
        return 0.5 * jnp.tanh(s) - 0.25 * jnp.tanh(q) + shift

    own_row = own_ids[...]
    own_col = as_column(own_row)

    w = weigh(far[...], near[...], own_col, own_row)
    total[...] = fold(w)
    wb = w.astype(jnp.bfloat16)
    acc_far[...] = dot_nn(wb, near[:, :ds])
    acc_near[...] = dot_tn(wb, far[:, :ds])

    rows_of = [pl.ds(i * each, each) for i in range(CHUNKS)]
    pf_copies = [
        remote(pf_out.at[rows], pf_in.at[rows], pf_send.at[i], pf_recv.at[i], at_blk(far_from))
        for i, rows in enumerate(rows_of)
    ]
    pn_copies = [
        remote(pn_out.at[rows], pn_in.at[rows], pn_send.at[i], pn_recv.at[i], at_blk(near_from))
        for i, rows in enumerate(rows_of)
    ]
    s1 = [
        remote(
            stage1_own, stage1.at[b], s1_send.at[k - 1], s1_recv.at[k - 1],
            at_blk(lax.rem(b + k, n_blk)),
        )
        for k in range(1, n_blk)
    ]

    def share_total():
        stage1_own[...] = total[...]
        stage1[pl.ds(b, 1)] = total[...][None]
        for c in s1:
            c.start()

    far_side = (far, far_in, ids_f, far_ids_in, far_copies, acc_far, pf_out, pf_copies)
    near_side = (near, near_in, ids_n, near_ids_in, near_copies, acc_near, pn_out, pn_copies)

    def process(early, late):
        e_own, e_in, e_ids, e_ids_in, e_copies, e_acc, e_out, e_back = early
        l_own, l_in, l_ids, l_ids_in, l_copies, l_acc, l_out, l_back = late
        e_ids.wait_recv()
        e_row = e_ids_in[...]
        e_col = as_column(e_row)
        for i, rows in enumerate(rows_of):
            e_copies[i].wait_recv()
            x = e_in[rows, :]
            w = weigh(x, l_own[...], e_col[i * each : (i + 1) * each], own_row)
            total[...] += fold(w)
            w = w.astype(jnp.bfloat16)
            l_acc[...] += dot_tn(w, x[:, :ds])
            part[rows, :] = dot_nn(w, l_own[:, :ds])
        l_ids.wait_recv()
        l_col = as_column(l_ids_in[...])
        for i, rows in enumerate(rows_of):
            l_copies[i].wait_recv()
            x = l_in[rows, :]
            x_id = l_col[i * each : (i + 1) * each]
            w1 = weigh(x, e_own[...], x_id, own_row)
            w2 = weigh(x, e_in[...], x_id, e_row)
            total[...] += fold(w1) + fold(w2)
            if i == CHUNKS - 1:
                share_total()
            w1 = w1.astype(jnp.bfloat16)
            w2 = w2.astype(jnp.bfloat16)
            back = dot_nn(w1, e_own[:, :ds]) + dot_nn(w2, e_in[:, :ds])
            l_out[rows, :] = (back * scale_s).astype(jnp.bfloat16)
            l_back[i].start()
            e_acc[...] += dot_tn(w1, x[:, :ds])
            part[...] += dot_tn(w2, x[:, :ds])
        for i, rows in enumerate(rows_of):
            e_out[rows, :] = (part[rows, :] * scale_s).astype(jnp.bfloat16)
            e_back[i].start()

    process(far_side, near_side)

    def finish(copies, acc, arrived):
        for c, rows in zip(copies, rows_of):
            c.wait_recv()
            acc[rows, :] = acc[rows, :] * scale_s + arrived[rows, :].astype(jnp.float32)

    finish(pn_copies, acc_near, pn_in)
    for c in s1:
        c.wait_recv()
    total_blk = stage1[0]
    for k in range(1, n_blk):
        total_blk = total_blk + stage1[k]
    stage2_own[...] = total_blk
    stage2[pl.ds(g, 1)] = total_blk[None]
    s2 = []
    for k in range(1, n_grp):
        c = remote(
            stage2_own, stage2.at[g], s2_send.at[k - 1], s2_recv.at[k - 1],
            {"blk": b, "grp": lax.rem(g + k, n_grp)},
        )
        c.start()
        s2.append(c)
    finish(pf_copies, acc_far, pf_in)

    for c in s2:
        c.wait_recv()
    whole = stage2[0]
    for k in range(1, n_grp):
        whole = whole + stage2[k]
    out_bias[...] = jnp.full((1, 1), jnp.sum(whole) * inv_count, jnp.float32)

    for c in [ids_f, ids_n] + near_copies + far_copies + pf_copies + pn_copies + s1 + s2:
        c.wait_send()


def land(of_far, of_near, bias, out_img, out_txt, out_bias, sems):
    role = lax.rem(lax.axis_index("grp"), 2)

    def put(a, b):
        return [
            pltpu.make_async_copy(a, out_img, sems.at[0]),
            pltpu.make_async_copy(b, out_txt, sems.at[1]),
        ]

    @pl.when(role == 0)
    def _():
        for c in put(of_near, of_far):
            c.start()

    @pl.when(role == 1)
    def _():
        for c in put(of_far, of_near):
            c.start()

    put_bias = pltpu.make_async_copy(bias, out_bias, sems.at[2])
    put_bias.start()
    put_bias.wait()
    for c in put(of_near, of_far):
        c.wait()


def solution(mesh):
    n_blk, n_grp = mesh.shape["blk"], mesh.shape["grp"]

    def body(image_student, image_teacher, text_student, text_teacher, pair_ids):
        size, ds = image_student.shape[2:]
        dt = image_teacher.shape[3]
        bf, f32 = jnp.bfloat16, jnp.float32
        dma = lambda k: pltpu.SemaphoreType.DMA((max(k, 1),))
        count = float(n_blk * n_grp * WINDOW * size * size)
        far, near, bias = pl.pallas_call(
            functools.partial(kernel, n_blk, n_grp, ds, 1.0 / count),
            out_shape=(
                jax.ShapeDtypeStruct((size, ds), f32),
                jax.ShapeDtypeStruct((size, ds), f32),
                jax.ShapeDtypeStruct((1, 1), f32),
            ),
            in_specs=[pl.BlockSpec(memory_space=pl.ANY)] * 5,
            out_specs=(
                pl.BlockSpec(memory_space=pltpu.VMEM),
                pl.BlockSpec(memory_space=pltpu.VMEM),
                pl.BlockSpec(memory_space=pltpu.VMEM),
            ),
            scratch_shapes=[
                pltpu.VMEM((size, ds + dt), bf),
                pltpu.VMEM((size, ds + dt), bf),
                pltpu.VMEM((1, size), jnp.int32),
                pltpu.VMEM((size, ds + dt), bf),
                pltpu.VMEM((size, ds + dt), bf),
                pltpu.VMEM((1, size), jnp.int32),
                pltpu.VMEM((1, size), jnp.int32),
                pltpu.VMEM((size, ds), f32),
                pltpu.VMEM((size, ds), bf),
                pltpu.VMEM((size, ds), bf),
                pltpu.VMEM((size, ds), bf),
                pltpu.VMEM((size, ds), bf),
                pltpu.VMEM((8, 128), f32),
                pltpu.VMEM((8, 128), f32),
                pltpu.VMEM((n_blk, 8, 128), f32),
                pltpu.VMEM((8, 128), f32),
                pltpu.VMEM((n_grp, 8, 128), f32),
                dma(5),
                dma(CHUNKS),
                dma(CHUNKS),
                dma(CHUNKS),
                dma(CHUNKS),
                dma(2),
                dma(2),
                dma(CHUNKS),
                dma(CHUNKS),
                dma(CHUNKS),
                dma(CHUNKS),
                dma(n_blk - 1),
                dma(n_blk - 1),
                dma(n_grp - 1),
                dma(n_grp - 1),
                pltpu.SemaphoreType.REGULAR,
                pltpu.SemaphoreType.REGULAR,
            ],
            compiler_params=pltpu.CompilerParams(
                collective_id=0, has_side_effects=True, vmem_limit_bytes=30 * 1024 * 1024
            ),
        )(
            *(
                pltpu.with_memory_space_constraint(x, pltpu.HBM)
                for x in (
                    image_student[0, 0],
                    image_teacher[0, 0],
                    text_student[0, 0],
                    text_teacher[0, 0],
                    pair_ids[0],
                )
            )
        )
        img, txt, bias = pl.pallas_call(
            land,
            out_shape=(
                jax.ShapeDtypeStruct((size, ds), f32),
                jax.ShapeDtypeStruct((size, ds), f32),
                jax.ShapeDtypeStruct((1, 1), f32),
            ),
            in_specs=[pl.BlockSpec(memory_space=pltpu.VMEM)] * 3,
            out_specs=[pl.BlockSpec(memory_space=pl.ANY)] * 3,
            scratch_shapes=[dma(3)],
            compiler_params=pltpu.CompilerParams(vmem_limit_bytes=30 * 1024 * 1024),
        )(far, near, bias)
        return img[None, None], txt[None, None], bias[0, 0]

    return jax.shard_map(
        body,
        mesh=mesh,
        in_specs=(
            P("blk", "grp", None, None),
            P("blk", "grp", None, None),
            P("blk", "grp", None, None),
            P("blk", "grp", None, None),
            P("blk", "grp", None),
        ),
        out_specs=(P("blk", "grp", None, None), P("blk", "grp", None, None), P()),
        check_vma=False,
    )
```

```python
import functools
import math

import jax
import jax.numpy as jnp
from jax import lax
from jax.experimental import pallas as pl
from jax.experimental.pallas import tpu as pltpu
from jax.sharding import PartitionSpec as P

MESH = pl.DeviceIdType.MESH
WINDOW = 4
FAR = 2
NEAR = 2
PLAIN = ("nnff", "")
NEAR_WRAPS = ("ff", "nn")
FAR_WRAPS = ("", "ffnn")


def dot_nt(a, b):
    return lax.dot_general(a, b, (((1,), (1,)), ((), ())), preferred_element_type=jnp.float32)


def dot_tn(a, b):
    return lax.dot_general(a, b, (((0,), (0,)), ((), ())), preferred_element_type=jnp.float32)


def dot_nn(a, b):
    return jnp.dot(a, b, preferred_element_type=jnp.float32)


def fold(w):
    w = jnp.sum(w.reshape(w.shape[0] // 8, 8, w.shape[1]), axis=0)
    out = w[:, 0:128]
    for at in range(128, w.shape[1], 128):
        out = out + w[:, at : at + 128]
    return out


def kernel(
    n_blk,
    n_grp,
    ds,
    img_stu,
    img_tea,
    txt_stu,
    txt_tea,
    ids,
    acc_far,
    acc_near,
    out_total,
    far,
    near,
    own_ids,
    far_in,
    near_in,
    far_ids_in,
    near_ids_in,
    part,
    pf_out,
    pn_out,
    pf_in,
    pn_in,
    total,
    stage1_own,
    stage1,
    stage2_own,
    stage2,
    local_sem,
    far_send,
    far_recv,
    near_send,
    near_recv,
    ids_send,
    ids_recv,
    pf_send,
    pf_recv,
    pn_send,
    pn_recv,
    s1_send,
    s1_recv,
    s2_send,
    s2_recv,
    up_sem,
    down_sem,
):
    b = lax.axis_index("blk")
    g = lax.axis_index("grp")
    size = far.shape[0]
    dt = far.shape[1] - ds
    role = lax.rem(g, 2)
    step = 1 - 2 * role
    far_to = lax.rem(b + 2 * step + 2 * n_blk, n_blk)
    far_from = lax.rem(b - 2 * step + 2 * n_blk, n_blk)
    near_to = lax.rem(b - step + n_blk, n_blk)
    near_from = lax.rem(b + step + n_blk, n_blk)

    def at_blk(i):
        return {"blk": i, "grp": g}

    def loads(f_stu, f_tea, n_stu, n_tea):
        return [
            pltpu.make_async_copy(f_stu, far.at[:, pl.ds(0, ds)], local_sem.at[0]),
            pltpu.make_async_copy(f_tea, far.at[:, pl.ds(ds, dt)], local_sem.at[1]),
            pltpu.make_async_copy(n_stu, near.at[:, pl.ds(0, ds)], local_sem.at[2]),
            pltpu.make_async_copy(n_tea, near.at[:, pl.ds(ds, dt)], local_sem.at[3]),
        ]

    @pl.when(role == 0)
    def _():
        for c in loads(txt_stu, txt_tea, img_stu, img_tea):
            c.start()

    @pl.when(role == 1)
    def _():
        for c in loads(img_stu, img_tea, txt_stu, txt_tea):
            c.start()

    ids_load = pltpu.make_async_copy(ids, own_ids, local_sem.at[4])
    ids_load.start()

    has_up, has_down = b + 2 < n_blk, b >= 2
    links = ((1, b + 1 < n_blk), (2, has_up), (-1, b >= 1), (-2, has_down))
    barrier = pltpu.get_barrier_semaphore()
    expected = jnp.int32(n_grp - 1)
    for offset, present in links:
        expected = expected + present.astype(jnp.int32)

        @pl.when(present)
        def _():
            pl.semaphore_signal(
                barrier, inc=1, device_id=at_blk(b + offset), device_id_type=MESH
            )

    for k in range(1, n_grp):
        pl.semaphore_signal(
            barrier,
            inc=1,
            device_id={"blk": b, "grp": lax.rem(g + k, n_grp)},
            device_id_type=MESH,
        )
    for c in loads(txt_stu, txt_tea, img_stu, img_tea):
        c.wait()
    ids_load.wait()
    pl.semaphore_wait(barrier, expected)

    def remote(src, dst, send, recv, to):
        return pltpu.make_async_remote_copy(
            src_ref=src, dst_ref=dst, send_sem=send, recv_sem=recv,
            device_id=to, device_id_type=MESH,
        )

    def pieces(n):
        return [(pl.ds(i * (size // n), size // n), slice(i * (size // n), (i + 1) * (size // n))) for i in range(n)]

    far_rows, near_rows = pieces(FAR), pieces(NEAR)
    ids_f = remote(own_ids, far_ids_in, ids_send.at[0], ids_recv.at[0], at_blk(far_to))
    ids_n = remote(own_ids, near_ids_in, ids_send.at[1], ids_recv.at[1], at_blk(near_to))
    near_copies = [
        remote(
            near.at[rows], near_in.at[rows],
            near_send.at[j], near_recv.at[j], at_blk(near_to),
        )
        for j, (rows, _) in enumerate(near_rows)
    ]
    far_copies = [
        remote(
            far.at[rows], far_in.at[rows],
            far_send.at[i], far_recv.at[i], at_blk(far_to),
        )
        for i, (rows, _) in enumerate(far_rows)
    ]
    near_wraps = jnp.where(role == 0, b == 0, b == n_blk - 1)
    far_wraps = jnp.where(role == 0, jnp.logical_not(has_up), jnp.logical_not(has_down))

    def begin(order, done=""):
        sent = {"n": done.count("n"), "f": done.count("f")}
        for kind in order:
            ids_copy, copies = (ids_n, near_copies) if kind == "n" else (ids_f, far_copies)
            if sent[kind] == 0:
                ids_copy.start()
            copies[sent[kind]].start()
            sent[kind] += 1

    plain = jnp.logical_not(jnp.logical_or(near_wraps, far_wraps))
    cases = ((plain, PLAIN), (near_wraps, NEAR_WRAPS), (far_wraps, FAR_WRAPS))
    for case, (at_once, _) in cases:

        @pl.when(case)
        def _():
            begin(at_once)

    def tell(sem, offset):
        pl.semaphore_signal(sem, inc=1, device_id=at_blk(b + offset), device_id_type=MESH)

    def pass_up():
        @pl.when(has_down)
        def _():
            pl.semaphore_wait(up_sem, 1)

        @pl.when(has_up)
        def _():
            tell(up_sem, 2)

    def pass_down():
        @pl.when(has_up)
        def _():
            pl.semaphore_wait(down_sem, 1)

        @pl.when(has_down)
        def _():
            tell(down_sem, -2)

    lower = b < n_blk // 2

    @pl.when(lower)
    def _():
        pass_up()
        pass_down()

    @pl.when(jnp.logical_not(lower))
    def _():
        pass_down()
        pass_up()

    for case, (at_once, after) in cases:

        @pl.when(case)
        def _():
            begin(after, at_once)

    scale_s = 2.0 / math.sqrt(ds)
    scale_t = 2.0 / math.sqrt(dt)

    def as_column(row):
        return jnp.transpose(jnp.broadcast_to(row, (128, row.shape[1])))[:, 0:1]

    def weigh(f, n, f_id, n_id):
        s = dot_nt(f[:, :ds], n[:, :ds]) * (0.5 * scale_s) - 0.5
        q = dot_nt(f[:, ds:], n[:, ds:]) * (0.5 * scale_t) - 0.5
        shift = jnp.where(f_id == n_id, -0.25, 0.25)
        return 0.5 * jnp.tanh(s) - 0.25 * jnp.tanh(q) + shift

    own_row = own_ids[...]
    own_col = as_column(own_row)

    w = weigh(far[...], near[...], own_col, own_row)
    total[...] = fold(w)
    wb = w.astype(jnp.bfloat16)
    acc_far[...] = dot_nn(wb, near[:, :ds])
    acc_near[...] = dot_tn(wb, far[:, :ds])

    pf_copies = [
        remote(pf_out.at[rows], pf_in.at[rows], pf_send.at[i], pf_recv.at[i], at_blk(far_from))
        for i, (rows, _) in enumerate(far_rows)
    ]
    pn_copies = [
        remote(pn_out.at[rows], pn_in.at[rows], pn_send.at[i], pn_recv.at[i], at_blk(near_from))
        for i, (rows, _) in enumerate(near_rows)
    ]
    s1 = [
        remote(
            stage1_own, stage1.at[b], s1_send.at[k - 1], s1_recv.at[k - 1],
            at_blk(lax.rem(b + k, n_blk)),
        )
        for k in range(1, n_blk)
    ]

    def share_total():
        stage1_own[...] = total[...]
        stage1[pl.ds(b, 1)] = total[...][None]
        for c in s1:
            c.start()

    far_side = (far, far_in, ids_f, far_ids_in, far_copies, acc_far, pf_out, pf_copies, far_rows)
    near_side = (near, near_in, ids_n, near_ids_in, near_copies, acc_near, pn_out, pn_copies, near_rows)

    def process(early, late):
        e_own, e_in, e_ids, e_ids_in, e_copies, e_acc, e_out, e_back, e_rows = early
        l_own, l_in, l_ids, l_ids_in, l_copies, l_acc, l_out, l_back, l_rows = late
        e_ids.wait_recv()
        e_row = e_ids_in[...]
        e_col = as_column(e_row)
        for i, (rows, span) in enumerate(e_rows):
            e_copies[i].wait_recv()
            x = e_in[rows, :]
            w = weigh(x, l_own[...], e_col[span], own_row)
            total[...] += fold(w)
            w = w.astype(jnp.bfloat16)
            l_acc[...] += dot_tn(w, x[:, :ds])
            part[rows, :] = dot_nn(w, l_own[:, :ds])
        l_ids.wait_recv()
        l_col = as_column(l_ids_in[...])
        for i, (rows, span) in enumerate(l_rows):
            l_copies[i].wait_recv()
            x = l_in[rows, :]
            x_id = l_col[span]
            w1 = weigh(x, e_own[...], x_id, own_row)
            w2 = weigh(x, e_in[...], x_id, e_row)
            total[...] += fold(w1) + fold(w2)
            if i == len(l_rows) - 1:
                share_total()
            w1 = w1.astype(jnp.bfloat16)
            w2 = w2.astype(jnp.bfloat16)
            back = dot_nn(w1, e_own[:, :ds]) + dot_nn(w2, e_in[:, :ds])
            l_out[rows, :] = (back * scale_s).astype(jnp.bfloat16)
            l_back[i].start()
            e_acc[...] += dot_tn(w1, x[:, :ds])
            part[...] += dot_tn(w2, x[:, :ds])
        for i, (rows, _) in enumerate(e_rows):
            e_out[rows, :] = (part[rows, :] * scale_s).astype(jnp.bfloat16)
            e_back[i].start()

    process(far_side, near_side)

    def finish(copies, acc, arrived, pieces):
        for c, (rows, _) in zip(copies, pieces):
            c.wait_recv()
            acc[rows, :] = acc[rows, :] * scale_s + arrived[rows, :].astype(jnp.float32)

    for c in s1:
        c.wait_recv()
    total_blk = stage1[0]
    for k in range(1, n_blk):
        total_blk = total_blk + stage1[k]
    stage2_own[...] = total_blk
    stage2[pl.ds(g, 1)] = total_blk[None]
    s2 = []
    for k in range(1, n_grp):
        c = remote(
            stage2_own, stage2.at[g], s2_send.at[k - 1], s2_recv.at[k - 1],
            {"blk": b, "grp": lax.rem(g + k, n_grp)},
        )
        c.start()
        s2.append(c)
    finish(pn_copies, acc_near, pn_in, near_rows)
    finish(pf_copies, acc_far, pf_in, far_rows)

    for c in s2:
        c.wait_recv()
    whole = stage2[0]
    for k in range(1, n_grp):
        whole = whole + stage2[k]
    out_total[...] = whole

    for c in [ids_f, ids_n] + near_copies + far_copies + pf_copies + pn_copies + s1 + s2:
        c.wait_send()


def land(inv_count, of_far, of_near, total, out_img, out_txt, out_bias, mean, sems):
    role = lax.rem(lax.axis_index("grp"), 2)

    def put(a, b):
        return [
            pltpu.make_async_copy(a, out_img, sems.at[0]),
            pltpu.make_async_copy(b, out_txt, sems.at[1]),
        ]

    @pl.when(role == 0)
    def _():
        for c in put(of_near, of_far):
            c.start()

    @pl.when(role == 1)
    def _():
        for c in put(of_far, of_near):
            c.start()

    mean[...] = jnp.full((1, 1), jnp.sum(total[...]) * inv_count, jnp.float32)
    put_bias = pltpu.make_async_copy(mean, out_bias, sems.at[2])
    put_bias.start()
    put_bias.wait()
    for c in put(of_near, of_far):
        c.wait()


def solution(mesh):
    n_blk, n_grp = mesh.shape["blk"], mesh.shape["grp"]

    def body(image_student, image_teacher, text_student, text_teacher, pair_ids):
        size, ds = image_student.shape[2:]
        dt = image_teacher.shape[3]
        bf, f32 = jnp.bfloat16, jnp.float32
        dma = lambda k: pltpu.SemaphoreType.DMA((max(k, 1),))
        count = float(n_blk * n_grp * WINDOW * size * size)
        far, near, total = pl.pallas_call(
            functools.partial(kernel, n_blk, n_grp, ds),
            out_shape=(
                jax.ShapeDtypeStruct((size, ds), f32),
                jax.ShapeDtypeStruct((size, ds), f32),
                jax.ShapeDtypeStruct((8, 128), f32),
            ),
            in_specs=[pl.BlockSpec(memory_space=pl.ANY)] * 5,
            out_specs=(
                pl.BlockSpec(memory_space=pltpu.VMEM),
                pl.BlockSpec(memory_space=pltpu.VMEM),
                pl.BlockSpec(memory_space=pltpu.VMEM),
            ),
            scratch_shapes=[
                pltpu.VMEM((size, ds + dt), bf),
                pltpu.VMEM((size, ds + dt), bf),
                pltpu.VMEM((1, size), jnp.int32),
                pltpu.VMEM((size, ds + dt), bf),
                pltpu.VMEM((size, ds + dt), bf),
                pltpu.VMEM((1, size), jnp.int32),
                pltpu.VMEM((1, size), jnp.int32),
                pltpu.VMEM((size, ds), f32),
                pltpu.VMEM((size, ds), bf),
                pltpu.VMEM((size, ds), bf),
                pltpu.VMEM((size, ds), bf),
                pltpu.VMEM((size, ds), bf),
                pltpu.VMEM((8, 128), f32),
                pltpu.VMEM((8, 128), f32),
                pltpu.VMEM((n_blk, 8, 128), f32),
                pltpu.VMEM((8, 128), f32),
                pltpu.VMEM((n_grp, 8, 128), f32),
                dma(5),
                dma(FAR),
                dma(FAR),
                dma(NEAR),
                dma(NEAR),
                dma(2),
                dma(2),
                dma(FAR),
                dma(FAR),
                dma(NEAR),
                dma(NEAR),
                dma(n_blk - 1),
                dma(n_blk - 1),
                dma(n_grp - 1),
                dma(n_grp - 1),
                pltpu.SemaphoreType.REGULAR,
                pltpu.SemaphoreType.REGULAR,
            ],
            compiler_params=pltpu.CompilerParams(
                collective_id=0, has_side_effects=True, vmem_limit_bytes=30 * 1024 * 1024
            ),
        )(
            *(
                pltpu.with_memory_space_constraint(x, pltpu.HBM)
                for x in (
                    image_student[0, 0],
                    image_teacher[0, 0],
                    text_student[0, 0],
                    text_teacher[0, 0],
                    pair_ids[0],
                )
            )
        )
        img, txt, bias = pl.pallas_call(
            functools.partial(land, 1.0 / count),
            out_shape=(
                jax.ShapeDtypeStruct((size, ds), f32),
                jax.ShapeDtypeStruct((size, ds), f32),
                jax.ShapeDtypeStruct((1, 1), f32),
            ),
            in_specs=[pl.BlockSpec(memory_space=pltpu.VMEM)] * 3,
            out_specs=[pl.BlockSpec(memory_space=pl.ANY)] * 3,
            scratch_shapes=[pltpu.VMEM((1, 1), f32), dma(3)],
            compiler_params=pltpu.CompilerParams(vmem_limit_bytes=30 * 1024 * 1024),
        )(far, near, total)
        return img[None, None], txt[None, None], bias[0, 0]

    return jax.shard_map(
        body,
        mesh=mesh,
        in_specs=(
            P("blk", "grp", None, None),
            P("blk", "grp", None, None),
            P("blk", "grp", None, None),
            P("blk", "grp", None, None),
            P("blk", "grp", None),
        ),
        out_specs=(P("blk", "grp", None, None), P("blk", "grp", None, None), P()),
        check_vma=False,
    )
```

```python
import functools
import math

import jax
import jax.numpy as jnp
from jax import lax
from jax.experimental import pallas as pl
from jax.experimental.pallas import tpu as pltpu
from jax.sharding import PartitionSpec as P

MESH = pl.DeviceIdType.MESH
WINDOW = 4
FAR = (2, 2)
NEAR = (9, 7)
PLAIN = ("nnff", "")
NEAR_WRAPS = ("ff", "nn")
FAR_WRAPS = ("", "ffnn")


def dot_nt(a, b):
    return lax.dot_general(a, b, (((1,), (1,)), ((), ())), preferred_element_type=jnp.float32)


def dot_tn(a, b):
    return lax.dot_general(a, b, (((0,), (0,)), ((), ())), preferred_element_type=jnp.float32)


def dot_nn(a, b):
    return jnp.dot(a, b, preferred_element_type=jnp.float32)


def fold(w):
    w = jnp.sum(w.reshape(w.shape[0] // 8, 8, w.shape[1]), axis=0)
    out = w[:, 0:128]
    for at in range(128, w.shape[1], 128):
        out = out + w[:, at : at + 128]
    return out


def kernel(
    n_blk,
    n_grp,
    ds,
    img_stu,
    img_tea,
    txt_stu,
    txt_tea,
    ids,
    acc_far,
    acc_near,
    out_total,
    far,
    near,
    own_ids,
    far_in,
    near_in,
    far_ids_in,
    near_ids_in,
    part,
    pf_out,
    pn_out,
    pf_in,
    pn_in,
    total,
    stage1_own,
    stage1,
    stage2_own,
    stage2,
    local_sem,
    far_send,
    far_recv,
    near_send,
    near_recv,
    ids_send,
    ids_recv,
    pf_send,
    pf_recv,
    pn_send,
    pn_recv,
    s1_send,
    s1_recv,
    s2_send,
    s2_recv,
    up_sem,
    down_sem,
):
    b = lax.axis_index("blk")
    g = lax.axis_index("grp")
    size = far.shape[0]
    dt = far.shape[1] - ds
    role = lax.rem(g, 2)
    step = 1 - 2 * role
    far_to = lax.rem(b + 2 * step + 2 * n_blk, n_blk)
    far_from = lax.rem(b - 2 * step + 2 * n_blk, n_blk)
    near_to = lax.rem(b - step + n_blk, n_blk)
    near_from = lax.rem(b + step + n_blk, n_blk)

    def at_blk(i):
        return {"blk": i, "grp": g}

    def loads(f_stu, f_tea, n_stu, n_tea):
        return [
            pltpu.make_async_copy(f_stu, far.at[:, pl.ds(0, ds)], local_sem.at[0]),
            pltpu.make_async_copy(f_tea, far.at[:, pl.ds(ds, dt)], local_sem.at[1]),
            pltpu.make_async_copy(n_stu, near.at[:, pl.ds(0, ds)], local_sem.at[2]),
            pltpu.make_async_copy(n_tea, near.at[:, pl.ds(ds, dt)], local_sem.at[3]),
        ]

    @pl.when(role == 0)
    def _():
        for c in loads(txt_stu, txt_tea, img_stu, img_tea):
            c.start()

    @pl.when(role == 1)
    def _():
        for c in loads(img_stu, img_tea, txt_stu, txt_tea):
            c.start()

    ids_load = pltpu.make_async_copy(ids, own_ids, local_sem.at[4])
    ids_load.start()

    has_up, has_down = b + 2 < n_blk, b >= 2
    links = ((1, b + 1 < n_blk), (2, has_up), (-1, b >= 1), (-2, has_down))
    barrier = pltpu.get_barrier_semaphore()
    expected = jnp.int32(n_grp - 1)
    for offset, present in links:
        expected = expected + present.astype(jnp.int32)

        @pl.when(present)
        def _():
            pl.semaphore_signal(
                barrier, inc=1, device_id=at_blk(b + offset), device_id_type=MESH
            )

    for k in range(1, n_grp):
        pl.semaphore_signal(
            barrier,
            inc=1,
            device_id={"blk": b, "grp": lax.rem(g + k, n_grp)},
            device_id_type=MESH,
        )
    pl.semaphore_wait(barrier, expected)

    def tell(sem, offset):
        pl.semaphore_signal(sem, inc=1, device_id=at_blk(b + offset), device_id_type=MESH)

    @pl.when(jnp.logical_not(has_down))
    def _():
        tell(up_sem, 2)

    @pl.when(jnp.logical_not(has_up))
    def _():
        tell(down_sem, -2)

    for c in loads(txt_stu, txt_tea, img_stu, img_tea):
        c.wait()
    ids_load.wait()

    def remote(src, dst, send, recv, to):
        return pltpu.make_async_remote_copy(
            src_ref=src, dst_ref=dst, send_sem=send, recv_sem=recv,
            device_id=to, device_id_type=MESH,
        )

    def pieces(parts):
        unit, at, out = size // sum(parts), 0, []
        for part in parts:
            out.append((pl.ds(at, part * unit), slice(at, at + part * unit)))
            at += part * unit
        return out

    far_rows, near_rows = pieces(FAR), pieces(NEAR)
    ids_f = remote(own_ids, far_ids_in, ids_send.at[0], ids_recv.at[0], at_blk(far_to))
    ids_n = remote(own_ids, near_ids_in, ids_send.at[1], ids_recv.at[1], at_blk(near_to))
    near_copies = [
        remote(
            near.at[rows], near_in.at[rows],
            near_send.at[j], near_recv.at[j], at_blk(near_to),
        )
        for j, (rows, _) in enumerate(near_rows)
    ]
    far_copies = [
        remote(
            far.at[rows], far_in.at[rows],
            far_send.at[i], far_recv.at[i], at_blk(far_to),
        )
        for i, (rows, _) in enumerate(far_rows)
    ]
    near_wraps = jnp.where(role == 0, b == 0, b == n_blk - 1)
    far_wraps = jnp.where(role == 0, jnp.logical_not(has_up), jnp.logical_not(has_down))

    def begin(order, done=""):
        sent = {"n": done.count("n"), "f": done.count("f")}
        for kind in order:
            ids_copy, copies = (ids_n, near_copies) if kind == "n" else (ids_f, far_copies)
            if sent[kind] == 0:
                ids_copy.start()
            copies[sent[kind]].start()
            sent[kind] += 1

    plain = jnp.logical_not(jnp.logical_or(near_wraps, far_wraps))
    is_last = jnp.where(role == 0, b == n_blk - 1, b == 0)
    cases = (
        (plain, PLAIN), (near_wraps, NEAR_WRAPS),
        (jnp.logical_and(far_wraps, jnp.logical_not(is_last)), FAR_WRAPS),
        (jnp.logical_and(far_wraps, is_last), ('n', 'ffn')),
    )
    for case, (at_once, _) in cases:

        @pl.when(case)
        def _():
            begin(at_once)

    def pass_up():
        @pl.when(has_down)
        def _():
            pl.semaphore_wait(up_sem, 1)

        @pl.when(jnp.logical_and(has_down, has_up))
        def _():
            tell(up_sem, 2)

    def pass_down():
        @pl.when(has_up)
        def _():
            pl.semaphore_wait(down_sem, 1)

        @pl.when(jnp.logical_and(has_down, has_up))
        def _():
            tell(down_sem, -2)

    lower = b < n_blk // 2

    @pl.when(lower)
    def _():
        pass_up()
        pass_down()

    @pl.when(jnp.logical_not(lower))
    def _():
        pass_down()
        pass_up()

    for case, (at_once, after) in cases:

        @pl.when(case)
        def _():
            begin(after, at_once)

    scale_s = 2.0 / math.sqrt(ds)
    scale_t = 2.0 / math.sqrt(dt)

    def as_column(row):
        return jnp.transpose(jnp.broadcast_to(row, (128, row.shape[1])))[:, 0:1]

    def weigh(f, n, f_id, n_id):
        s = dot_nt(f[:, :ds], n[:, :ds]) * (0.5 * scale_s) - 0.5
        q = dot_nt(f[:, ds:], n[:, ds:]) * (0.5 * scale_t) - 0.5
        shift = jnp.where(f_id == n_id, -0.25, 0.25)
        return 0.5 * jnp.tanh(s) - 0.25 * jnp.tanh(q) + shift

    own_row = own_ids[...]
    own_col = as_column(own_row)

    w = weigh(far[...], near[...], own_col, own_row)
    total[...] = fold(w)
    wb = w.astype(jnp.bfloat16)
    acc_far[...] = dot_nn(wb, near[:, :ds])
    acc_near[...] = dot_tn(wb, far[:, :ds])

    pf_copies = [
        remote(pf_out.at[rows], pf_in.at[rows], pf_send.at[i], pf_recv.at[i], at_blk(far_from))
        for i, (rows, _) in enumerate(far_rows)
    ]
    pn_copies = [
        remote(pn_out.at[rows], pn_in.at[rows], pn_send.at[i], pn_recv.at[i], at_blk(near_from))
        for i, (rows, _) in enumerate(near_rows)
    ]
    s1 = [
        remote(
            stage1_own, stage1.at[b], s1_send.at[k - 1], s1_recv.at[k - 1],
            at_blk(lax.rem(b + k, n_blk)),
        )
        for k in range(1, n_blk)
    ]

    def share_total():
        stage1_own[...] = total[...]
        stage1[pl.ds(b, 1)] = total[...][None]
        for c in s1:
            c.start()

    far_side = (far, far_in, ids_f, far_ids_in, far_copies, acc_far, pf_out, pf_copies, far_rows)
    near_side = (near, near_in, ids_n, near_ids_in, near_copies, acc_near, pn_out, pn_copies, near_rows)

    def process(early, late):
        e_own, e_in, e_ids, e_ids_in, e_copies, e_acc, e_out, e_back, e_rows = early
        l_own, l_in, l_ids, l_ids_in, l_copies, l_acc, l_out, l_back, l_rows = late
        e_ids.wait_recv()
        e_row = e_ids_in[...]
        e_col = as_column(e_row)
        for i, (rows, span) in enumerate(e_rows):
            e_copies[i].wait_recv()
            x = e_in[rows, :]
            w = weigh(x, l_own[...], e_col[span], own_row)
            total[...] += fold(w)
            w = w.astype(jnp.bfloat16)
            l_acc[...] += dot_tn(w, x[:, :ds])
            part[rows, :] = dot_nn(w, l_own[:, :ds])
        l_ids.wait_recv()
        l_col = as_column(l_ids_in[...])
        for i, (rows, span) in enumerate(l_rows):
            l_copies[i].wait_recv()
            x = l_in[rows, :]
            x_id = l_col[span]
            w1 = weigh(x, e_own[...], x_id, own_row)
            w2 = weigh(x, e_in[...], x_id, e_row)
            total[...] += fold(w1) + fold(w2)
            if i == len(l_rows) - 1:
                share_total()
            w1 = w1.astype(jnp.bfloat16)
            w2 = w2.astype(jnp.bfloat16)
            back = dot_nn(w1, e_own[:, :ds]) + dot_nn(w2, e_in[:, :ds])
            l_out[rows, :] = (back * scale_s).astype(jnp.bfloat16)
            l_back[i].start()
            part[...] += dot_tn(w2, x[:, :ds])
            if i == len(l_rows) - 1:
                for c, (back_rows, _) in zip(e_back, e_rows):
                    e_out[back_rows, :] = (part[back_rows, :] * scale_s).astype(jnp.bfloat16)
                    c.start()
            e_acc[...] += dot_tn(w1, x[:, :ds])

    process(far_side, near_side)

    def finish(copies, acc, arrived, pieces):
        for c, (rows, _) in zip(copies, pieces):
            c.wait_recv()
            acc[rows, :] = acc[rows, :] * scale_s + arrived[rows, :].astype(jnp.float32)

    for c in s1:
        c.wait_recv()
    total_blk = stage1[0]
    for k in range(1, n_blk):
        total_blk = total_blk + stage1[k]
    stage2_own[...] = total_blk
    stage2[pl.ds(g, 1)] = total_blk[None]
    s2 = []
    for k in range(1, n_grp):
        c = remote(
            stage2_own, stage2.at[g], s2_send.at[k - 1], s2_recv.at[k - 1],
            {"blk": b, "grp": lax.rem(g + k, n_grp)},
        )
        c.start()
        s2.append(c)
    finish(pn_copies, acc_near, pn_in, near_rows)
    finish(pf_copies, acc_far, pf_in, far_rows)

    for c in s2:
        c.wait_recv()
    whole = stage2[0]
    for k in range(1, n_grp):
        whole = whole + stage2[k]
    out_total[...] = whole

    for c in [ids_f, ids_n] + near_copies + far_copies + pf_copies + pn_copies + s1 + s2:
        c.wait_send()


def land(inv_count, of_far, of_near, total, out_img, out_txt, out_bias, mean, sems):
    role = lax.rem(lax.axis_index("grp"), 2)

    def put(a, b):
        return [
            pltpu.make_async_copy(a, out_img, sems.at[0]),
            pltpu.make_async_copy(b, out_txt, sems.at[1]),
        ]

    @pl.when(role == 0)
    def _():
        for c in put(of_near, of_far):
            c.start()

    @pl.when(role == 1)
    def _():
        for c in put(of_far, of_near):
            c.start()

    mean[...] = jnp.full((1, 1), jnp.sum(total[...]) * inv_count, jnp.float32)
    put_bias = pltpu.make_async_copy(mean, out_bias, sems.at[2])
    put_bias.start()
    put_bias.wait()
    for c in put(of_near, of_far):
        c.wait()


def solution(mesh):
    n_blk, n_grp = mesh.shape["blk"], mesh.shape["grp"]

    def body(image_student, image_teacher, text_student, text_teacher, pair_ids):
        size, ds = image_student.shape[2:]
        dt = image_teacher.shape[3]
        bf, f32 = jnp.bfloat16, jnp.float32
        dma = lambda k: pltpu.SemaphoreType.DMA((max(k, 1),))
        count = float(n_blk * n_grp * WINDOW * size * size)
        far, near, total = pl.pallas_call(
            functools.partial(kernel, n_blk, n_grp, ds),
            out_shape=(
                jax.ShapeDtypeStruct((size, ds), f32),
                jax.ShapeDtypeStruct((size, ds), f32),
                jax.ShapeDtypeStruct((8, 128), f32),
            ),
            in_specs=[pl.BlockSpec(memory_space=pl.ANY)] * 5,
            out_specs=(
                pl.BlockSpec(memory_space=pltpu.VMEM),
                pl.BlockSpec(memory_space=pltpu.VMEM),
                pl.BlockSpec(memory_space=pltpu.VMEM),
            ),
            scratch_shapes=[
                pltpu.VMEM((size, ds + dt), bf),
                pltpu.VMEM((size, ds + dt), bf),
                pltpu.VMEM((1, size), jnp.int32),
                pltpu.VMEM((size, ds + dt), bf),
                pltpu.VMEM((size, ds + dt), bf),
                pltpu.VMEM((1, size), jnp.int32),
                pltpu.VMEM((1, size), jnp.int32),
                pltpu.VMEM((size, ds), f32),
                pltpu.VMEM((size, ds), bf),
                pltpu.VMEM((size, ds), bf),
                pltpu.VMEM((size, ds), bf),
                pltpu.VMEM((size, ds), bf),
                pltpu.VMEM((8, 128), f32),
                pltpu.VMEM((8, 128), f32),
                pltpu.VMEM((n_blk, 8, 128), f32),
                pltpu.VMEM((8, 128), f32),
                pltpu.VMEM((n_grp, 8, 128), f32),
                dma(5),
                dma(len(FAR)),
                dma(len(FAR)),
                dma(len(NEAR)),
                dma(len(NEAR)),
                dma(2),
                dma(2),
                dma(len(FAR)),
                dma(len(FAR)),
                dma(len(NEAR)),
                dma(len(NEAR)),
                dma(n_blk - 1),
                dma(n_blk - 1),
                dma(n_grp - 1),
                dma(n_grp - 1),
                pltpu.SemaphoreType.REGULAR,
                pltpu.SemaphoreType.REGULAR,
            ],
            compiler_params=pltpu.CompilerParams(
                collective_id=0, has_side_effects=True, vmem_limit_bytes=30 * 1024 * 1024
            ),
        )(
            *(
                pltpu.with_memory_space_constraint(x, pltpu.HBM)
                for x in (
                    image_student[0, 0],
                    image_teacher[0, 0],
                    text_student[0, 0],
                    text_teacher[0, 0],
                    pair_ids[0],
                )
            )
        )
        img, txt, bias = pl.pallas_call(
            functools.partial(land, 1.0 / count),
            out_shape=(
                jax.ShapeDtypeStruct((size, ds), f32),
                jax.ShapeDtypeStruct((size, ds), f32),
                jax.ShapeDtypeStruct((1, 1), f32),
            ),
            in_specs=[pl.BlockSpec(memory_space=pltpu.VMEM)] * 3,
            out_specs=[pl.BlockSpec(memory_space=pl.ANY)] * 3,
            scratch_shapes=[pltpu.VMEM((1, 1), f32), dma(3)],
            compiler_params=pltpu.CompilerParams(vmem_limit_bytes=30 * 1024 * 1024),
        )(far, near, total)
        return img[None, None], txt[None, None], bias[0, 0]

    return jax.shard_map(
        body,
        mesh=mesh,
        in_specs=(
            P("blk", "grp", None, None),
            P("blk", "grp", None, None),
            P("blk", "grp", None, None),
            P("blk", "grp", None, None),
            P("blk", "grp", None),
        ),
        out_specs=(P("blk", "grp", None, None), P("blk", "grp", None, None), P()),
        check_vma=False,
    )
```

```python
import functools
import math

import jax
import jax.numpy as jnp
from jax import lax
from jax.experimental import pallas as pl
from jax.experimental.pallas import tpu as pltpu
from jax.sharding import PartitionSpec as P

MESH = pl.DeviceIdType.MESH
WINDOW = 4
FAR = 1
NEAR = 2
PLAIN = ("nnf", "")
NEAR_WRAPS = ("f", "nn")
FAR_WRAPS = ("", "fnn")


def dot_nt(a, b):
    return lax.dot_general(a, b, (((1,), (1,)), ((), ())), preferred_element_type=jnp.float32)


def dot_tn(a, b):
    return lax.dot_general(a, b, (((0,), (0,)), ((), ())), preferred_element_type=jnp.float32)


def dot_nn(a, b):
    return jnp.dot(a, b, preferred_element_type=jnp.float32)


def fold(w):
    w = jnp.sum(w.reshape(w.shape[0] // 8, 8, w.shape[1]), axis=0)
    out = w[:, 0:128]
    for at in range(128, w.shape[1], 128):
        out = out + w[:, at : at + 128]
    return out


def kernel(
    n_blk,
    n_grp,
    ds,
    img_stu,
    img_tea,
    txt_stu,
    txt_tea,
    ids,
    acc_far,
    acc_near,
    out_total,
    far,
    near,
    own_ids,
    far_in,
    near_in,
    far_ids_in,
    near_ids_in,
    part,
    pf_out,
    pn_out,
    pf_in,
    pn_in,
    total,
    stage1_own,
    stage1,
    stage2_own,
    stage2,
    local_sem,
    far_send,
    far_recv,
    near_send,
    near_recv,
    ids_send,
    ids_recv,
    pf_send,
    pf_recv,
    pn_send,
    pn_recv,
    s1_send,
    s1_recv,
    s2_send,
    s2_recv,
    up_sem,
    down_sem,
):
    b = lax.axis_index("blk")
    g = lax.axis_index("grp")
    size = far.shape[0]
    dt = far.shape[1] - ds
    role = lax.rem(g, 2)
    step = 1 - 2 * role
    far_to = lax.rem(b + 2 * step + 2 * n_blk, n_blk)
    far_from = lax.rem(b - 2 * step + 2 * n_blk, n_blk)
    near_to = lax.rem(b - step + n_blk, n_blk)
    near_from = lax.rem(b + step + n_blk, n_blk)

    def at_blk(i):
        return {"blk": i, "grp": g}

    def loads(f_stu, f_tea, n_stu, n_tea):
        return [
            pltpu.make_async_copy(f_stu, far.at[:, pl.ds(0, ds)], local_sem.at[0]),
            pltpu.make_async_copy(f_tea, far.at[:, pl.ds(ds, dt)], local_sem.at[1]),
            pltpu.make_async_copy(n_stu, near.at[:, pl.ds(0, ds)], local_sem.at[2]),
            pltpu.make_async_copy(n_tea, near.at[:, pl.ds(ds, dt)], local_sem.at[3]),
        ]

    @pl.when(role == 0)
    def _():
        for c in loads(txt_stu, txt_tea, img_stu, img_tea):
            c.start()

    @pl.when(role == 1)
    def _():
        for c in loads(img_stu, img_tea, txt_stu, txt_tea):
            c.start()

    ids_load = pltpu.make_async_copy(ids, own_ids, local_sem.at[4])
    ids_load.start()

    has_up, has_down = b + 2 < n_blk, b >= 2
    links = ((1, b + 1 < n_blk), (2, has_up), (-1, b >= 1), (-2, has_down))
    barrier = pltpu.get_barrier_semaphore()
    expected = jnp.int32(n_grp - 1)
    for offset, present in links:
        expected = expected + present.astype(jnp.int32)

        @pl.when(present)
        def _():
            pl.semaphore_signal(
                barrier, inc=1, device_id=at_blk(b + offset), device_id_type=MESH
            )

    for k in range(1, n_grp):
        pl.semaphore_signal(
            barrier,
            inc=1,
            device_id={"blk": b, "grp": lax.rem(g + k, n_grp)},
            device_id_type=MESH,
        )
    for c in loads(txt_stu, txt_tea, img_stu, img_tea):
        c.wait()
    ids_load.wait()
    pl.semaphore_wait(barrier, expected)

    def remote(src, dst, send, recv, to):
        return pltpu.make_async_remote_copy(
            src_ref=src, dst_ref=dst, send_sem=send, recv_sem=recv,
            device_id=to, device_id_type=MESH,
        )

    def pieces(n):
        return [(pl.ds(i * (size // n), size // n), slice(i * (size // n), (i + 1) * (size // n))) for i in range(n)]

    far_rows, near_rows = pieces(FAR), pieces(NEAR)
    ids_f = remote(own_ids, far_ids_in, ids_send.at[0], ids_recv.at[0], at_blk(far_to))
    ids_n = remote(own_ids, near_ids_in, ids_send.at[1], ids_recv.at[1], at_blk(near_to))
    near_copies = [
        remote(
            near.at[rows], near_in.at[rows],
            near_send.at[j], near_recv.at[j], at_blk(near_to),
        )
        for j, (rows, _) in enumerate(near_rows)
    ]
    far_copies = [
        remote(
            far.at[rows], far_in.at[rows],
            far_send.at[i], far_recv.at[i], at_blk(far_to),
        )
        for i, (rows, _) in enumerate(far_rows)
    ]
    near_wraps = jnp.where(role == 0, b == 0, b == n_blk - 1)
    far_wraps = jnp.where(role == 0, jnp.logical_not(has_up), jnp.logical_not(has_down))

    def begin(order, done=""):
        sent = {"n": done.count("n"), "f": done.count("f")}
        for kind in order:
            ids_copy, copies = (ids_n, near_copies) if kind == "n" else (ids_f, far_copies)
            if sent[kind] == 0:
                ids_copy.start()
            copies[sent[kind]].start()
            sent[kind] += 1

    plain = jnp.logical_not(jnp.logical_or(near_wraps, far_wraps))
    cases = ((plain, PLAIN), (near_wraps, NEAR_WRAPS), (far_wraps, FAR_WRAPS))
    for case, (at_once, _) in cases:

        @pl.when(case)
        def _():
            begin(at_once)

    def tell(sem, offset):
        pl.semaphore_signal(sem, inc=1, device_id=at_blk(b + offset), device_id_type=MESH)

    def pass_up():
        @pl.when(has_down)
        def _():
            pl.semaphore_wait(up_sem, 1)

        @pl.when(has_up)
        def _():
            tell(up_sem, 2)

    def pass_down():
        @pl.when(has_up)
        def _():
            pl.semaphore_wait(down_sem, 1)

        @pl.when(has_down)
        def _():
            tell(down_sem, -2)

    lower = b < n_blk // 2

    @pl.when(lower)
    def _():
        pass_up()
        pass_down()

    @pl.when(jnp.logical_not(lower))
    def _():
        pass_down()
        pass_up()

    for case, (at_once, after) in cases:

        @pl.when(case)
        def _():
            begin(after, at_once)

    scale_s = 2.0 / math.sqrt(ds)
    scale_t = 2.0 / math.sqrt(dt)

    def as_column(row):
        return jnp.transpose(jnp.broadcast_to(row, (128, row.shape[1])))[:, 0:1]

    def weigh(f, n, f_id, n_id):
        s = dot_nt(f[:, :ds], n[:, :ds]) * (0.5 * scale_s) - 0.5
        q = dot_nt(f[:, ds:], n[:, ds:]) * (0.5 * scale_t) - 0.5
        shift = jnp.where(f_id == n_id, -0.25, 0.25)
        return 0.5 * jnp.tanh(s) - 0.25 * jnp.tanh(q) + shift

    own_row = own_ids[...]
    own_col = as_column(own_row)

    w = weigh(far[...], near[...], own_col, own_row)
    total[...] = fold(w)
    wb = w.astype(jnp.bfloat16)
    acc_far[...] = dot_nn(wb, near[:, :ds])
    acc_near[...] = dot_tn(wb, far[:, :ds])

    pf_copies = [
        remote(pf_out.at[rows], pf_in.at[rows], pf_send.at[i], pf_recv.at[i], at_blk(far_from))
        for i, (rows, _) in enumerate(far_rows)
    ]
    pn_copies = [
        remote(pn_out.at[rows], pn_in.at[rows], pn_send.at[i], pn_recv.at[i], at_blk(near_from))
        for i, (rows, _) in enumerate(near_rows)
    ]
    s1 = [
        remote(
            stage1_own, stage1.at[b], s1_send.at[k - 1], s1_recv.at[k - 1],
            at_blk(lax.rem(b + k, n_blk)),
        )
        for k in range(1, n_blk)
    ]

    def share_total():
        stage1_own[...] = total[...]
        stage1[pl.ds(b, 1)] = total[...][None]
        for c in s1:
            c.start()

    far_side = (far, far_in, ids_f, far_ids_in, far_copies, acc_far, pf_out, pf_copies, far_rows)
    near_side = (near, near_in, ids_n, near_ids_in, near_copies, acc_near, pn_out, pn_copies, near_rows)

    def process(early, late):
        e_own, e_in, e_ids, e_ids_in, e_copies, e_acc, e_out, e_back, e_rows = early
        l_own, l_in, l_ids, l_ids_in, l_copies, l_acc, l_out, l_back, l_rows = late
        e_ids.wait_recv()
        e_row = e_ids_in[...]
        e_col = as_column(e_row)
        for i, (rows, span) in enumerate(e_rows):
            e_copies[i].wait_recv()
            x = e_in[rows, :]
            w = weigh(x, l_own[...], e_col[span], own_row)
            total[...] += fold(w)
            w = w.astype(jnp.bfloat16)
            l_acc[...] += dot_tn(w, x[:, :ds])
            part[rows, :] = dot_nn(w, l_own[:, :ds])
        l_ids.wait_recv()
        l_col = as_column(l_ids_in[...])
        for i, (rows, span) in enumerate(l_rows):
            l_copies[i].wait_recv()
            x = l_in[rows, :]
            x_id = l_col[span]
            w1 = weigh(x, e_own[...], x_id, own_row)
            w2 = weigh(x, e_in[...], x_id, e_row)
            total[...] += fold(w1) + fold(w2)
            if i == len(l_rows) - 1:
                share_total()
            w1 = w1.astype(jnp.bfloat16)
            w2 = w2.astype(jnp.bfloat16)
            back = dot_nn(w1, e_own[:, :ds]) + dot_nn(w2, e_in[:, :ds])
            l_out[rows, :] = (back * scale_s).astype(jnp.bfloat16)
            l_back[i].start()
            e_acc[...] += dot_tn(w1, x[:, :ds])
            part[...] += dot_tn(w2, x[:, :ds])
        for i, (rows, _) in enumerate(e_rows):
            e_out[rows, :] = (part[rows, :] * scale_s).astype(jnp.bfloat16)
            e_back[i].start()

    process(far_side, near_side)

    def finish(copies, acc, arrived, pieces):
        for c, (rows, _) in zip(copies, pieces):
            c.wait_recv()
            acc[rows, :] = acc[rows, :] * scale_s + arrived[rows, :].astype(jnp.float32)

    for c in s1:
        c.wait_recv()
    total_blk = stage1[0]
    for k in range(1, n_blk):
        total_blk = total_blk + stage1[k]
    stage2_own[...] = total_blk
    stage2[pl.ds(g, 1)] = total_blk[None]
    s2 = []
    for k in range(1, n_grp):
        c = remote(
            stage2_own, stage2.at[g], s2_send.at[k - 1], s2_recv.at[k - 1],
            {"blk": b, "grp": lax.rem(g + k, n_grp)},
        )
        c.start()
        s2.append(c)
    finish(pn_copies, acc_near, pn_in, near_rows)
    finish(pf_copies, acc_far, pf_in, far_rows)

    for c in s2:
        c.wait_recv()
    whole = stage2[0]
    for k in range(1, n_grp):
        whole = whole + stage2[k]
    out_total[...] = whole

    for c in [ids_f, ids_n] + near_copies + far_copies + pf_copies + pn_copies + s1 + s2:
        c.wait_send()


def land(inv_count, of_far, of_near, total, out_img, out_txt, out_bias, mean, sems):
    role = lax.rem(lax.axis_index("grp"), 2)

    def put(a, b):
        return [
            pltpu.make_async_copy(a, out_img, sems.at[0]),
            pltpu.make_async_copy(b, out_txt, sems.at[1]),
        ]

    @pl.when(role == 0)
    def _():
        for c in put(of_near, of_far):
            c.start()

    @pl.when(role == 1)
    def _():
        for c in put(of_far, of_near):
            c.start()

    mean[...] = jnp.full((1, 1), jnp.sum(total[...]) * inv_count, jnp.float32)
    put_bias = pltpu.make_async_copy(mean, out_bias, sems.at[2])
    put_bias.start()
    put_bias.wait()
    for c in put(of_near, of_far):
        c.wait()


def solution(mesh):
    n_blk, n_grp = mesh.shape["blk"], mesh.shape["grp"]

    def body(image_student, image_teacher, text_student, text_teacher, pair_ids):
        size, ds = image_student.shape[2:]
        dt = image_teacher.shape[3]
        bf, f32 = jnp.bfloat16, jnp.float32
        dma = lambda k: pltpu.SemaphoreType.DMA((max(k, 1),))
        count = float(n_blk * n_grp * WINDOW * size * size)
        far, near, total = pl.pallas_call(
            functools.partial(kernel, n_blk, n_grp, ds),
            out_shape=(
                jax.ShapeDtypeStruct((size, ds), f32),
                jax.ShapeDtypeStruct((size, ds), f32),
                jax.ShapeDtypeStruct((8, 128), f32),
            ),
            in_specs=[pl.BlockSpec(memory_space=pl.ANY)] * 5,
            out_specs=(
                pl.BlockSpec(memory_space=pltpu.VMEM),
                pl.BlockSpec(memory_space=pltpu.VMEM),
                pl.BlockSpec(memory_space=pltpu.VMEM),
            ),
            scratch_shapes=[
                pltpu.VMEM((size, ds + dt), bf),
                pltpu.VMEM((size, ds + dt), bf),
                pltpu.VMEM((1, size), jnp.int32),
                pltpu.VMEM((size, ds + dt), bf),
                pltpu.VMEM((size, ds + dt), bf),
                pltpu.VMEM((1, size), jnp.int32),
                pltpu.VMEM((1, size), jnp.int32),
                pltpu.VMEM((size, ds), f32),
                pltpu.VMEM((size, ds), bf),
                pltpu.VMEM((size, ds), bf),
                pltpu.VMEM((size, ds), bf),
                pltpu.VMEM((size, ds), bf),
                pltpu.VMEM((8, 128), f32),
                pltpu.VMEM((8, 128), f32),
                pltpu.VMEM((n_blk, 8, 128), f32),
                pltpu.VMEM((8, 128), f32),
                pltpu.VMEM((n_grp, 8, 128), f32),
                dma(5),
                dma(FAR),
                dma(FAR),
                dma(NEAR),
                dma(NEAR),
                dma(2),
                dma(2),
                dma(FAR),
                dma(FAR),
                dma(NEAR),
                dma(NEAR),
                dma(n_blk - 1),
                dma(n_blk - 1),
                dma(n_grp - 1),
                dma(n_grp - 1),
                pltpu.SemaphoreType.REGULAR,
                pltpu.SemaphoreType.REGULAR,
            ],
            compiler_params=pltpu.CompilerParams(
                collective_id=0, has_side_effects=True, vmem_limit_bytes=30 * 1024 * 1024
            ),
        )(
            *(
                pltpu.with_memory_space_constraint(x, pltpu.HBM)
                for x in (
                    image_student[0, 0],
                    image_teacher[0, 0],
                    text_student[0, 0],
                    text_teacher[0, 0],
                    pair_ids[0],
                )
            )
        )
        img, txt, bias = pl.pallas_call(
            functools.partial(land, 1.0 / count),
            out_shape=(
                jax.ShapeDtypeStruct((size, ds), f32),
                jax.ShapeDtypeStruct((size, ds), f32),
                jax.ShapeDtypeStruct((1, 1), f32),
            ),
            in_specs=[pl.BlockSpec(memory_space=pltpu.VMEM)] * 3,
            out_specs=[pl.BlockSpec(memory_space=pl.ANY)] * 3,
            scratch_shapes=[pltpu.VMEM((1, 1), f32), dma(3)],
            compiler_params=pltpu.CompilerParams(vmem_limit_bytes=30 * 1024 * 1024),
        )(far, near, total)
        return img[None, None], txt[None, None], bias[0, 0]

    return jax.shard_map(
        body,
        mesh=mesh,
        in_specs=(
            P("blk", "grp", None, None),
            P("blk", "grp", None, None),
            P("blk", "grp", None, None),
            P("blk", "grp", None, None),
            P("blk", "grp", None),
        ),
        out_specs=(P("blk", "grp", None, None), P("blk", "grp", None, None), P()),
        check_vma=False,
    )
```

```python
import functools
import math

import jax
import jax.numpy as jnp
from jax import lax
from jax.experimental import pallas as pl
from jax.experimental.pallas import tpu as pltpu
from jax.sharding import PartitionSpec as P

MESH = pl.DeviceIdType.MESH
WINDOW = 4
FAR = 2
NEAR = 2
PLAIN = ("nnff", "")
NEAR_WRAPS = ("ff", "nn")
FAR_WRAPS = ("", "ffnn")
LAST = ("nn", "ff")


def dot_nt(a, b):
    return lax.dot_general(a, b, (((1,), (1,)), ((), ())), preferred_element_type=jnp.float32)


def dot_tn(a, b):
    return lax.dot_general(a, b, (((0,), (0,)), ((), ())), preferred_element_type=jnp.float32)


def dot_nn(a, b):
    return jnp.dot(a, b, preferred_element_type=jnp.float32)


def fold(w):
    w = jnp.sum(w.reshape(w.shape[0] // 8, 8, w.shape[1]), axis=0)
    out = w[:, 0:128]
    for at in range(128, w.shape[1], 128):
        out = out + w[:, at : at + 128]
    return out


def kernel(
    n_blk,
    n_grp,
    ds,
    img_stu,
    img_tea,
    txt_stu,
    txt_tea,
    ids,
    acc_far,
    acc_near,
    out_total,
    far,
    near,
    own_ids,
    far_in,
    near_in,
    far_ids_in,
    near_ids_in,
    part,
    pf_out,
    pn_out,
    pf_in,
    pn_in,
    total,
    stage1_own,
    stage1,
    stage2_own,
    stage2,
    local_sem,
    far_send,
    far_recv,
    near_send,
    near_recv,
    ids_send,
    ids_recv,
    pf_send,
    pf_recv,
    pn_send,
    pn_recv,
    s1_send,
    s1_recv,
    s2_send,
    s2_recv,
    up_sem,
    down_sem,
):
    b = lax.axis_index("blk")
    g = lax.axis_index("grp")
    size = far.shape[0]
    dt = far.shape[1] - ds
    role = lax.rem(g, 2)
    step = 1 - 2 * role
    far_to = lax.rem(b + 2 * step + 2 * n_blk, n_blk)
    far_from = lax.rem(b - 2 * step + 2 * n_blk, n_blk)
    near_to = lax.rem(b - step + n_blk, n_blk)
    near_from = lax.rem(b + step + n_blk, n_blk)

    def at_blk(i):
        return {"blk": i, "grp": g}

    def loads(f_stu, f_tea, n_stu, n_tea):
        return [
            pltpu.make_async_copy(f_stu, far.at[:, pl.ds(0, ds)], local_sem.at[0]),
            pltpu.make_async_copy(f_tea, far.at[:, pl.ds(ds, dt)], local_sem.at[1]),
            pltpu.make_async_copy(n_stu, near.at[:, pl.ds(0, ds)], local_sem.at[2]),
            pltpu.make_async_copy(n_tea, near.at[:, pl.ds(ds, dt)], local_sem.at[3]),
        ]

    @pl.when(role == 0)
    def _():
        for c in loads(txt_stu, txt_tea, img_stu, img_tea):
            c.start()

    @pl.when(role == 1)
    def _():
        for c in loads(img_stu, img_tea, txt_stu, txt_tea):
            c.start()

    ids_load = pltpu.make_async_copy(ids, own_ids, local_sem.at[4])
    ids_load.start()

    has_up, has_down = b + 2 < n_blk, b >= 2
    links = ((1, b + 1 < n_blk), (2, has_up), (-1, b >= 1), (-2, has_down))
    barrier = pltpu.get_barrier_semaphore()
    expected = jnp.int32(n_grp - 1)
    for offset, present in links:
        expected = expected + present.astype(jnp.int32)

        @pl.when(present)
        def _():
            pl.semaphore_signal(
                barrier, inc=1, device_id=at_blk(b + offset), device_id_type=MESH
            )

    for k in range(1, n_grp):
        pl.semaphore_signal(
            barrier,
            inc=1,
            device_id={"blk": b, "grp": lax.rem(g + k, n_grp)},
            device_id_type=MESH,
        )
    for c in loads(txt_stu, txt_tea, img_stu, img_tea):
        c.wait()
    ids_load.wait()
    pl.semaphore_wait(barrier, expected)

    def remote(src, dst, send, recv, to):
        return pltpu.make_async_remote_copy(
            src_ref=src, dst_ref=dst, send_sem=send, recv_sem=recv,
            device_id=to, device_id_type=MESH,
        )

    def pieces(n):
        return [(pl.ds(i * (size // n), size // n), slice(i * (size // n), (i + 1) * (size // n))) for i in range(n)]

    far_rows, near_rows = pieces(FAR), pieces(NEAR)
    ids_f = remote(own_ids, far_ids_in, ids_send.at[0], ids_recv.at[0], at_blk(far_to))
    ids_n = remote(own_ids, near_ids_in, ids_send.at[1], ids_recv.at[1], at_blk(near_to))
    near_copies = [
        remote(
            near.at[rows], near_in.at[rows],
            near_send.at[j], near_recv.at[j], at_blk(near_to),
        )
        for j, (rows, _) in enumerate(near_rows)
    ]
    far_copies = [
        remote(
            far.at[rows], far_in.at[rows],
            far_send.at[i], far_recv.at[i], at_blk(far_to),
        )
        for i, (rows, _) in enumerate(far_rows)
    ]
    near_wraps = jnp.where(role == 0, b == 0, b == n_blk - 1)
    far_wraps = jnp.where(role == 0, jnp.logical_not(has_up), jnp.logical_not(has_down))

    def begin(order, done=""):
        sent = {"n": done.count("n"), "f": done.count("f")}
        for kind in order:
            ids_copy, copies = (ids_n, near_copies) if kind == "n" else (ids_f, far_copies)
            if sent[kind] == 0:
                ids_copy.start()
            copies[sent[kind]].start()
            sent[kind] += 1

    plain = jnp.logical_not(jnp.logical_or(near_wraps, far_wraps))
    is_last = jnp.where(role == 0, b == n_blk - 1, b == 0)
    cases = (
        (plain, PLAIN),
        (near_wraps, NEAR_WRAPS),
        (jnp.logical_and(far_wraps, jnp.logical_not(is_last)), FAR_WRAPS),
        (jnp.logical_and(far_wraps, is_last), LAST),
    )
    for case, (at_once, _) in cases:

        @pl.when(case)
        def _():
            begin(at_once)

    def tell(sem, offset):
        pl.semaphore_signal(sem, inc=1, device_id=at_blk(b + offset), device_id_type=MESH)

    def pass_up():
        @pl.when(has_down)
        def _():
            pl.semaphore_wait(up_sem, 1)

        @pl.when(has_up)
        def _():
            tell(up_sem, 2)

    def pass_down():
        @pl.when(has_up)
        def _():
            pl.semaphore_wait(down_sem, 1)

        @pl.when(has_down)
        def _():
            tell(down_sem, -2)

    lower = b < n_blk // 2

    @pl.when(lower)
    def _():
        pass_up()
        pass_down()

    @pl.when(jnp.logical_not(lower))
    def _():
        pass_down()
        pass_up()

    for case, (at_once, after) in cases:

        @pl.when(case)
        def _():
            begin(after, at_once)

    scale_s = 2.0 / math.sqrt(ds)
    scale_t = 2.0 / math.sqrt(dt)

    def as_column(row):
        return jnp.transpose(jnp.broadcast_to(row, (128, row.shape[1])))[:, 0:1]

    def weigh(f, n, f_id, n_id):
        s = dot_nt(f[:, :ds], n[:, :ds]) * (0.5 * scale_s) - 0.5
        q = dot_nt(f[:, ds:], n[:, ds:]) * (0.5 * scale_t) - 0.5
        shift = jnp.where(f_id == n_id, -0.25, 0.25)
        return 0.5 * jnp.tanh(s) - 0.25 * jnp.tanh(q) + shift

    own_row = own_ids[...]
    own_col = as_column(own_row)

    w = weigh(far[...], near[...], own_col, own_row)
    total[...] = fold(w)
    wb = w.astype(jnp.bfloat16)
    acc_far[...] = dot_nn(wb, near[:, :ds])
    acc_near[...] = dot_tn(wb, far[:, :ds])

    pf_copies = [
        remote(pf_out.at[rows], pf_in.at[rows], pf_send.at[i], pf_recv.at[i], at_blk(far_from))
        for i, (rows, _) in enumerate(far_rows)
    ]
    pn_copies = [
        remote(pn_out.at[rows], pn_in.at[rows], pn_send.at[i], pn_recv.at[i], at_blk(near_from))
        for i, (rows, _) in enumerate(near_rows)
    ]
    s1 = [
        remote(
            stage1_own, stage1.at[b], s1_send.at[k - 1], s1_recv.at[k - 1],
            at_blk(lax.rem(b + k, n_blk)),
        )
        for k in range(1, n_blk)
    ]

    def share_total():
        stage1_own[...] = total[...]
        stage1[pl.ds(b, 1)] = total[...][None]
        for c in s1:
            c.start()

    far_side = (far, far_in, ids_f, far_ids_in, far_copies, acc_far, pf_out, pf_copies, far_rows)
    near_side = (near, near_in, ids_n, near_ids_in, near_copies, acc_near, pn_out, pn_copies, near_rows)

    def process(early, late):
        e_own, e_in, e_ids, e_ids_in, e_copies, e_acc, e_out, e_back, e_rows = early
        l_own, l_in, l_ids, l_ids_in, l_copies, l_acc, l_out, l_back, l_rows = late
        e_ids.wait_recv()
        e_row = e_ids_in[...]
        e_col = as_column(e_row)
        for i, (rows, span) in enumerate(e_rows):
            e_copies[i].wait_recv()
            x = e_in[rows, :]
            w = weigh(x, l_own[...], e_col[span], own_row)
            total[...] += fold(w)
            w = w.astype(jnp.bfloat16)
            l_acc[...] += dot_tn(w, x[:, :ds])
            part[rows, :] = dot_nn(w, l_own[:, :ds])
        l_ids.wait_recv()
        l_col = as_column(l_ids_in[...])
        for i, (rows, span) in enumerate(l_rows):
            l_copies[i].wait_recv()
            x = l_in[rows, :]
            x_id = l_col[span]
            w1 = weigh(x, e_own[...], x_id, own_row)
            w2 = weigh(x, e_in[...], x_id, e_row)
            total[...] += fold(w1) + fold(w2)
            if i == len(l_rows) - 1:
                share_total()
            w1 = w1.astype(jnp.bfloat16)
            w2 = w2.astype(jnp.bfloat16)
            back = dot_nn(w1, e_own[:, :ds]) + dot_nn(w2, e_in[:, :ds])
            l_out[rows, :] = (back * scale_s).astype(jnp.bfloat16)
            l_back[i].start()
            e_acc[...] += dot_tn(w1, x[:, :ds])
            part[...] += dot_tn(w2, x[:, :ds])
        for i, (rows, _) in enumerate(e_rows):
            e_out[rows, :] = (part[rows, :] * scale_s).astype(jnp.bfloat16)
            e_back[i].start()

    process(far_side, near_side)

    def finish(copies, acc, arrived, pieces):
        for c, (rows, _) in zip(copies, pieces):
            c.wait_recv()
            acc[rows, :] = acc[rows, :] * scale_s + arrived[rows, :].astype(jnp.float32)

    for c in s1:
        c.wait_recv()
    total_blk = stage1[0]
    for k in range(1, n_blk):
        total_blk = total_blk + stage1[k]
    stage2_own[...] = total_blk
    stage2[pl.ds(g, 1)] = total_blk[None]
    s2 = []
    for k in range(1, n_grp):
        c = remote(
            stage2_own, stage2.at[g], s2_send.at[k - 1], s2_recv.at[k - 1],
            {"blk": b, "grp": lax.rem(g + k, n_grp)},
        )
        c.start()
        s2.append(c)
    finish(pn_copies, acc_near, pn_in, near_rows)
    finish(pf_copies, acc_far, pf_in, far_rows)

    for c in s2:
        c.wait_recv()
    whole = stage2[0]
    for k in range(1, n_grp):
        whole = whole + stage2[k]
    out_total[...] = whole

    for c in [ids_f, ids_n] + near_copies + far_copies + pf_copies + pn_copies + s1 + s2:
        c.wait_send()


def land(inv_count, of_far, of_near, total, out_img, out_txt, out_bias, mean, sems):
    role = lax.rem(lax.axis_index("grp"), 2)

    def put(a, b):
        return [
            pltpu.make_async_copy(a, out_img, sems.at[0]),
            pltpu.make_async_copy(b, out_txt, sems.at[1]),
        ]

    @pl.when(role == 0)
    def _():
        for c in put(of_near, of_far):
            c.start()

    @pl.when(role == 1)
    def _():
        for c in put(of_far, of_near):
            c.start()

    mean[...] = jnp.full((1, 1), jnp.sum(total[...]) * inv_count, jnp.float32)
    put_bias = pltpu.make_async_copy(mean, out_bias, sems.at[2])
    put_bias.start()
    put_bias.wait()
    for c in put(of_near, of_far):
        c.wait()


def solution(mesh):
    n_blk, n_grp = mesh.shape["blk"], mesh.shape["grp"]

    def body(image_student, image_teacher, text_student, text_teacher, pair_ids):
        size, ds = image_student.shape[2:]
        dt = image_teacher.shape[3]
        bf, f32 = jnp.bfloat16, jnp.float32
        dma = lambda k: pltpu.SemaphoreType.DMA((max(k, 1),))
        count = float(n_blk * n_grp * WINDOW * size * size)
        far, near, total = pl.pallas_call(
            functools.partial(kernel, n_blk, n_grp, ds),
            out_shape=(
                jax.ShapeDtypeStruct((size, ds), f32),
                jax.ShapeDtypeStruct((size, ds), f32),
                jax.ShapeDtypeStruct((8, 128), f32),
            ),
            in_specs=[pl.BlockSpec(memory_space=pl.ANY)] * 5,
            out_specs=(
                pl.BlockSpec(memory_space=pltpu.VMEM),
                pl.BlockSpec(memory_space=pltpu.VMEM),
                pl.BlockSpec(memory_space=pltpu.VMEM),
            ),
            scratch_shapes=[
                pltpu.VMEM((size, ds + dt), bf),
                pltpu.VMEM((size, ds + dt), bf),
                pltpu.VMEM((1, size), jnp.int32),
                pltpu.VMEM((size, ds + dt), bf),
                pltpu.VMEM((size, ds + dt), bf),
                pltpu.VMEM((1, size), jnp.int32),
                pltpu.VMEM((1, size), jnp.int32),
                pltpu.VMEM((size, ds), f32),
                pltpu.VMEM((size, ds), bf),
                pltpu.VMEM((size, ds), bf),
                pltpu.VMEM((size, ds), bf),
                pltpu.VMEM((size, ds), bf),
                pltpu.VMEM((8, 128), f32),
                pltpu.VMEM((8, 128), f32),
                pltpu.VMEM((n_blk, 8, 128), f32),
                pltpu.VMEM((8, 128), f32),
                pltpu.VMEM((n_grp, 8, 128), f32),
                dma(5),
                dma(FAR),
                dma(FAR),
                dma(NEAR),
                dma(NEAR),
                dma(2),
                dma(2),
                dma(FAR),
                dma(FAR),
                dma(NEAR),
                dma(NEAR),
                dma(n_blk - 1),
                dma(n_blk - 1),
                dma(n_grp - 1),
                dma(n_grp - 1),
                pltpu.SemaphoreType.REGULAR,
                pltpu.SemaphoreType.REGULAR,
            ],
            compiler_params=pltpu.CompilerParams(
                collective_id=0, has_side_effects=True, vmem_limit_bytes=30 * 1024 * 1024
            ),
        )(
            *(
                pltpu.with_memory_space_constraint(x, pltpu.HBM)
                for x in (
                    image_student[0, 0],
                    image_teacher[0, 0],
                    text_student[0, 0],
                    text_teacher[0, 0],
                    pair_ids[0],
                )
            )
        )
        img, txt, bias = pl.pallas_call(
            functools.partial(land, 1.0 / count),
            out_shape=(
                jax.ShapeDtypeStruct((size, ds), f32),
                jax.ShapeDtypeStruct((size, ds), f32),
                jax.ShapeDtypeStruct((1, 1), f32),
            ),
            in_specs=[pl.BlockSpec(memory_space=pltpu.VMEM)] * 3,
            out_specs=[pl.BlockSpec(memory_space=pl.ANY)] * 3,
            scratch_shapes=[pltpu.VMEM((1, 1), f32), dma(3)],
            compiler_params=pltpu.CompilerParams(vmem_limit_bytes=30 * 1024 * 1024),
        )(far, near, total)
        return img[None, None], txt[None, None], bias[0, 0]

    return jax.shard_map(
        body,
        mesh=mesh,
        in_specs=(
            P("blk", "grp", None, None),
            P("blk", "grp", None, None),
            P("blk", "grp", None, None),
            P("blk", "grp", None, None),
            P("blk", "grp", None),
        ),
        out_specs=(P("blk", "grp", None, None), P("blk", "grp", None, None), P()),
        check_vma=False,
    )
```
